32 devices in a mesh: vol: 1, slab: 8 (over z, x), filt: 4 (over y, core).
Axes of the slice: x: 2, y: 2, z: 4, core: 2. Of those that a mesh axis runs over, the one named last changes fastest.
Arguments:
- volume: bfloat16 [32, 64, 64, 256], P(('vol', 'slab', 'filt')), may hold values from -6 to 6
- weights: bfloat16 [256, 27, 256], P('filt'), may hold values from -0.078125 to 0.078125
- bias: bfloat16 [256], P('filt'), may hold values from -3 to 3
Outputs:
- activated: bfloat16 [32, 64, 64, 256], P(('vol', 'slab'), None, None, 'filt')
The draws below stay inside these ranges and needn't reach their ends.
All inputs are finite; a program needn't handle non-finite values.
Results may differ from the reference program's by a relative error of at most 0.001.
Values may be sent and summed in bfloat16 or wider, within the bound.
A program may use at most 448 MiB of HBM per device.

```python
import jax
import jax.numpy as jnp

C = 256
NY = 64
NX = 64
DEPTH = 32


def steps_of(own_key, extent, pieces, low, top_value):
    factor_of = 1.0
    for dim, blocks in pieces:
        heights = jax.random.uniform(jax.random.fold_in(jax.random.fold_in(own_key, 6), dim), (blocks,), jnp.float32, low / len(pieces), top_value / len(pieces))
        factor_of = factor_of * jnp.repeat(jnp.exp(heights), extent[dim] // blocks).reshape((-1,) + (1,) * (len(extent) - 1 - dim))
    return factor_of


def gaussian(rng, dims, deviation, limit, cuts=(), dtype=jnp.bfloat16):
    gain = steps_of(rng, dims, cuts, -0.22, 0.18) if cuts else 1.0
    entries = jax.random.normal(rng, dims, jnp.float32) * deviation * gain
    return jnp.minimum(jnp.maximum(entries, -limit), limit).astype(dtype)


def setup_inputs(seed: int = 0, part: int = 0) -> dict:
    key_of = jax.random.split(jax.random.key(seed), 4)
    part_splits = jax.random.split(jax.random.fold_in(key_of[3], part), 4)
    volume = gaussian(part_splits[0], (DEPTH, NY, NX, C), 1.0, 6.0, ((0, 32),))
    weights = gaussian(key_of[1], (C, 27, C), (27 * C) ** -0.5, 0.078125, ((0, 4),))
    bias = gaussian(key_of[2], (C,), 0.5, 3.0, ((0, 4),))
    return dict(volume=volume, weights=weights, bias=bias)


def reference(volume, weights, bias):
    depth, rows, cols, chans = volume.shape
    outs = weights.shape[0]
    padded = jnp.pad(volume, ((1, 1), (1, 1), (1, 1), (0, 0)))
    total = jnp.zeros((depth, rows * cols, outs), jnp.float32)
    for tap_z in range(3):
        for tap_y in range(3):
            for tap_x in range(3):
                window = padded[tap_z:tap_z + depth, tap_y:tap_y + rows, tap_x:tap_x + cols].reshape(depth, rows * cols, chans)
                tap_weight = weights[:, 9 * tap_z + 3 * tap_y + tap_x, :]
                total = total + jnp.einsum("zpi,oi->zpo", window.astype(jnp.float32), tap_weight.astype(jnp.float32))
    shifted = total + bias.astype(jnp.float32)[None, None, :]
    result = jnp.where(shifted > 0, shifted, 0.3 * shifted)
    return result.astype(jnp.bfloat16).reshape(depth, rows, cols, outs)
```

```python
import functools

import jax
import jax.numpy as jnp
from jax import lax
from jax.experimental import pallas as pl
from jax.experimental.pallas import tpu as pltpu
from jax.sharding import PartitionSpec as P

MESH = pl.DeviceIdType.MESH
LEAD = 4
HALO = 2


def kernel(slabs, vol_ref, w_hbm, b_hbm, out_ref, x, matrix, w_ref, b_ref, send, recv, local, params):
    rows, cols, chans = vol_ref.shape[1:]
    depth = out_ref.shape[0]
    outs = out_ref.shape[-1]
    last = rows // 2
    v = lax.axis_index("vol")
    s = lax.axis_index("slab")
    f = lax.axis_index("filt")
    odd = lax.rem(f, 2)
    mate = f + 1 - 2 * odd
    across = lax.rem(f + 2, 4)
    diag = 3 - f
    outer = (f == 0) | (f == 3)
    inner = ~outer
    has_prev = s > 0
    has_next = s < slabs - 1
    is_odd = odd == 1
    halo_to = s + 2 * odd - 1
    halo_in = 5 - 5 * odd
    mate_slot = 5 * odd
    sends_halo = (is_odd & has_next) | (~is_odd & has_prev)
    takes_halo = (is_odd & has_prev) | (~is_odd & has_next)

    to_across = (v, s, across)
    to_mate = (v, s, mate)
    to_halo = (v, halo_to, f)

    def on(k, act):
        edge = (k == 0) | (k == last)

        @pl.when((k > 0) & (k < last))
        def _():
            act(2 * k - 1, 2)

        @pl.when(edge)
        def _():
            act(jnp.where(k == 0, 0, rows - 1), 1)

    def own(lo, n):
        return vol_ref.at[0, pl.ds(lo, n)]

    def slot(z, lo, n):
        return x.at[z, pl.ds(lo + 1, n)]

    def remote(src, z, k, kind, dev, lo, n):
        return pltpu.make_async_remote_copy(
            src_ref=src,
            dst_ref=slot(z, lo, n),
            send_sem=send.at[kind],
            recv_sem=recv.at[z, k],
            device_id=dev,
            device_id_type=MESH,
        )

    def c_y(k, lo, n):
        return remote(own(lo, n), f + 1, k, 0, to_across, lo, n)

    def c_core(k, lo, n):
        return remote(own(lo, n), f + 1, k, 1, to_mate, lo, n)

    def c_fwd(k, lo, n):
        return remote(slot(across + 1, lo, n), across + 1, k, 2, to_mate, lo, n)

    def c_halo_own(k, lo, n):
        return remote(own(lo, n), halo_in, k, 3, to_halo, lo, n)

    def c_halo_fwd(k, lo, n):
        return remote(slot(across + 1, lo, n), halo_in, k, 3, to_halo, lo, n)

    def c_halo_mate(k, lo, n):
        return remote(slot(halo_in, lo, n), halo_in, k, 4, to_mate, lo, n)

    def c_local(k, lo, n):
        return pltpu.make_async_copy(own(lo, n), slot(f + 1, lo, n), local.at[k])

    def arrived(z, k, lo, n):
        remote(slot(z, lo, n), z, k, 0, to_mate, lo, n).wait_recv()

    get_w = pltpu.make_async_copy(w_hbm, w_ref, params.at[0])
    get_b = pltpu.make_async_copy(b_hbm, b_ref, params.at[1])
    get_w.start()
    get_b.start()

    barrier = pltpu.get_barrier_semaphore()
    pl.semaphore_signal(barrier, inc=1, device_id=to_mate, device_id_type=MESH)
    pl.semaphore_signal(barrier, inc=1, device_id=to_across, device_id_type=MESH)

    @pl.when(has_prev)
    def _():
        pl.semaphore_signal(barrier, inc=1, device_id=(v, s - 1, f), device_id_type=MESH)

    @pl.when(has_next)
    def _():
        pl.semaphore_signal(barrier, inc=1, device_id=(v, s + 1, f), device_id_type=MESH)

    both = has_prev & has_next

    @pl.when(both)
    def _():
        pl.semaphore_wait(barrier, 4)

    @pl.when(~both)
    def _():
        pl.semaphore_wait(barrier, 3)

    def send_outer(k):
        def go(lo, n):
            c_y(k, lo, n).start()

            @pl.when(sends_halo & (k < 6))
            def _():
                c_halo_own(k, lo, n).start()

        @pl.when(outer)
        def _():
            on(k, go)

    def send_inner(k):
        @pl.when(inner)
        def _():
            on(k, lambda lo, n: c_y(k, lo, n).start())

    def send_chip(k):
        def go(lo, n):
            c_core(k, lo, n).start()
            c_local(k, lo, n).start()

        on(k, go)

    def relay(k):
        def go(lo, n):
            arrived(across + 1, k, lo, n)
            c_fwd(k, lo, n).start()

            @pl.when(inner & sends_halo)
            def _():
                c_halo_fwd(k, lo, n).start()

        on(k, go)

    def relay_halo(k):
        def go(lo, n):
            arrived(halo_in, k, lo, n)
            c_halo_mate(k, lo, n).start()

        @pl.when(takes_halo)
        def _():
            on(k, go)

    def complete(k):
        def go(lo, n):
            c_local(k, lo, n).wait()
            arrived(mate + 1, k, lo, n)
            arrived(diag + 1, k, lo, n)

            @pl.when(sends_halo)
            def _():
                arrived(mate_slot, k, lo, n)

        on(k, go)

    @pl.loop(0, last + 1)
    def _(k):
        send_outer(k)
        send_chip(k)

    zero_row = jnp.zeros((cols, chans), x.dtype)
    for z in range(depth + 2):
        x[z, 0] = zero_row
        x[z, rows + 1] = zero_row

    def clear(z):
        @pl.loop(1, rows + 1)
        def _(r):
            x[z, r] = zero_row

    @pl.when(~has_prev)
    def _():
        clear(0)

    @pl.when(~has_next)
    def _():
        clear(depth + 1)

    get_w.wait()
    get_b.wait()
    for t in range(9):
        left, middle, right = (w_ref[3 * t + i] for i in range(3))
        tap = jnp.concatenate([middle, left, right, jnp.zeros_like(left)], axis=0)
        matrix[chans * t : chans * (t + 1)] = tap.T

    bias = b_ref[...].astype(jnp.float32)
    m = depth * 2 * cols
    place = lax.rem(lax.broadcasted_iota(jnp.int32, (m, 2 * outs), 0), cols)

    def compute(k):
        windows = [
            x[pl.ds(dz, depth), pl.ds(2 * k + dy, 2)].reshape(m, chans) for dz in range(3) for dy in range(3)
        ]
        total = jnp.dot(jnp.concatenate(windows, axis=1), matrix[...], preferred_element_type=jnp.float32)
        near = total[:, : 2 * outs]
        far = total[:, 2 * outs :]
        before = jnp.where(place == 0, 0.0, pltpu.roll(near, 1, 0))
        after = jnp.where(place == cols - 1, 0.0, pltpu.roll(far, m - 1, 0))
        full = near + after + pltpu.roll(before, outs, 1)
        shifted = full[:, :outs] + bias
        result = jnp.where(shifted > 0, shifted, 0.3 * shifted)
        out_ref[:, pl.ds(2 * k, 2)] = result.astype(out_ref.dtype).reshape(depth, 2, cols, outs)


    lead = jnp.where(inner, 10, 0)
    halo_lead = jnp.where(inner, 0, 0)

    @pl.loop(0, last + 2 + 2 + 10)
    def _(step):
        t = step - 10
        relay(t + lead)

        @pl.when(inner & (t == 0))
        def _():
            @pl.loop(0, last + 1)
            def _(k):
                send_inner(k)

        @pl.when(outer & sends_halo & (t + 6 >= 6))
        def _():
            on(t + 6, lambda lo, n: c_halo_own(t + 6, lo, n).start())

        relay_halo(t + halo_lead)
        complete(t - 2)

        @pl.when((t >= 3) & (t < last + 3))
        def _():
            compute(t - 3)

    whole = (0, rows)
    c_y(0, *whole).wait_send()
    c_core(0, *whole).wait_send()
    c_fwd(0, *whole).wait_send()

    @pl.when(sends_halo)
    def _():
        c_halo_own(0, *whole).wait_send()

    @pl.when(takes_halo)
    def _():
        c_halo_mate(0, *whole).wait_send()


def body(volume, weights, bias):
    planes, rows, cols, chans = volume.shape
    outs = weights.shape[0]
    slabs = lax.axis_size("slab")
    depth = planes * lax.axis_size("filt")
    chunks = rows // 2 + 1
    taps = weights.transpose(1, 0, 2)
    return pl.pallas_call(
        functools.partial(kernel, slabs),
        out_shape=pltpu.VMEM((depth, rows, cols, outs), jnp.bfloat16),
        in_specs=[
            pl.BlockSpec(memory_space=pltpu.HBM),
            pl.BlockSpec(memory_space=pltpu.HBM),
            pl.BlockSpec(memory_space=pltpu.HBM),
        ],
        out_specs=pl.BlockSpec(memory_space=pltpu.VMEM),
        scratch_shapes=[
            pltpu.VMEM((depth + 2, rows + 2, cols, chans), jnp.bfloat16),
            pltpu.VMEM((9 * chans, 4 * outs), jnp.bfloat16),
            pltpu.VMEM(taps.shape, jnp.bfloat16),
            pltpu.VMEM((1, outs), jnp.bfloat16),
            pltpu.SemaphoreType.DMA((5,)),
            pltpu.SemaphoreType.DMA((6, chunks)),
            pltpu.SemaphoreType.DMA((chunks,)),
            pltpu.SemaphoreType.DMA((2,)),
        ],
        compiler_params=pltpu.CompilerParams(
            collective_id=0, has_side_effects=True, vmem_limit_bytes=50 * 1024 * 1024
        ),
        cost_estimate=pl.CostEstimate(
            flops=2 * depth * rows * cols * outs * 27 * chans,
            bytes_accessed=16 * rows * cols * chans,
            transcendentals=0,
        ),
    )(volume, taps, bias.reshape(1, outs))


def solution(mesh):
    return jax.shard_map(
        body,
        mesh=mesh,
        in_specs=(P(("vol", "slab", "filt"), None, None, None), P("filt", None, None), P("filt")),
        out_specs=P(("vol", "slab"), None, None, "filt"),
        check_vma=False,
    )
```

```python
import functools

import jax
import jax.numpy as jnp
from jax import lax
from jax.experimental import pallas as pl
from jax.experimental.pallas import tpu as pltpu
from jax.sharding import PartitionSpec as P

MESH = pl.DeviceIdType.MESH
LEAD = 6
AHEAD = 6
TAIL = 3


def convolve(x, matrix, bias, k, depth):
    cols, chans = x.shape[2:]
    outs = bias.shape[-1]
    m = depth * 2 * cols
    windows = [x[pl.ds(dz, depth), pl.ds(2 * k + dy, 2)].reshape(m, chans) for dz in range(3) for dy in range(3)]
    total = jnp.dot(jnp.concatenate(windows, axis=1), matrix[...], preferred_element_type=jnp.float32)
    place = lax.rem(lax.broadcasted_iota(jnp.int32, (m, 2 * outs), 0), cols)
    near = total[:, : 2 * outs]
    far = total[:, 2 * outs :]
    before = jnp.where(place == 0, 0.0, pltpu.roll(near, 1, 0))
    after = jnp.where(place == cols - 1, 0.0, pltpu.roll(far, m - 1, 0))
    full = near + after + pltpu.roll(before, outs, 1)
    shifted = full[:, :outs] + bias
    result = jnp.where(shifted > 0, shifted, 0.3 * shifted)
    return result.astype(jnp.bfloat16).reshape(depth, 2, cols, outs)


def kernel(slabs, vol_ref, w_hbm, b_hbm, out_ref, x, matrix, b_ref, w_ref, send, recv, local, params):
    rows, cols, chans = vol_ref.shape[1:]
    depth = out_ref.shape[0]
    outs = out_ref.shape[-1]
    last = rows // 2
    v = lax.axis_index("vol")
    s = lax.axis_index("slab")
    f = lax.axis_index("filt")
    odd = lax.rem(f, 2)
    mate = f + 1 - 2 * odd
    across = lax.rem(f + 2, 4)
    diag = 3 - f
    outer = (f == 0) | (f == 3)
    inner = ~outer
    has_prev = s > 0
    has_next = s < slabs - 1
    is_odd = odd == 1
    halo_to = s + 2 * odd - 1
    halo_in = 5 - 5 * odd
    mate_slot = 5 * odd
    sends_halo = (is_odd & has_next) | (~is_odd & has_prev)
    takes_halo = (is_odd & has_prev) | (~is_odd & has_next)

    to_across = (v, s, across)
    to_mate = (v, s, mate)
    to_halo = (v, halo_to, f)

    def on(k, act):
        edge = (k == 0) | (k == last)

        @pl.when((k > 0) & (k < last))
        def _():
            act(2 * k - 1, 2)

        @pl.when(edge)
        def _():
            act(jnp.where(k == 0, 0, rows - 1), 1)

    def own(lo, n):
        return vol_ref.at[0, pl.ds(lo, n)]

    def slot(z, lo, n):
        return x.at[z, pl.ds(lo + 1, n)]

    def remote(src, z, k, kind, dev, lo, n):
        return pltpu.make_async_remote_copy(
            src_ref=src,
            dst_ref=slot(z, lo, n),
            send_sem=send.at[kind],
            recv_sem=recv.at[z, k],
            device_id=dev,
            device_id_type=MESH,
        )

    def c_y(k, lo, n):
        return remote(own(lo, n), f + 1, k, 0, to_across, lo, n)

    def c_core(k, lo, n):
        return remote(own(lo, n), f + 1, k, 1, to_mate, lo, n)

    def c_fwd(k, lo, n):
        return remote(slot(across + 1, lo, n), across + 1, k, 2, to_mate, lo, n)

    def c_halo_own(k, lo, n):
        return remote(own(lo, n), halo_in, k, 3, to_halo, lo, n)

    def c_halo_fwd(k, lo, n):
        return remote(slot(across + 1, lo, n), halo_in, k, 3, to_halo, lo, n)

    def c_halo_mate(k, lo, n):
        return remote(slot(halo_in, lo, n), halo_in, k, 4, to_mate, lo, n)

    def c_local(k, lo, n):
        return pltpu.make_async_copy(own(lo, n), slot(f + 1, lo, n), local.at[k])

    def arrived(z, k, lo, n):
        remote(slot(z, lo, n), z, k, 0, to_mate, lo, n).wait_recv()

    get_w = pltpu.make_async_copy(w_hbm, w_ref, params.at[0])
    get_b = pltpu.make_async_copy(b_hbm, b_ref, params.at[1])
    get_w.start()
    get_b.start()

    barrier = pltpu.get_barrier_semaphore()
    pl.semaphore_signal(barrier, inc=1, device_id=to_mate, device_id_type=MESH)
    pl.semaphore_signal(barrier, inc=1, device_id=to_across, device_id_type=MESH)

    @pl.when(has_prev)
    def _():
        pl.semaphore_signal(barrier, inc=1, device_id=(v, s - 1, f), device_id_type=MESH)

    @pl.when(has_next)
    def _():
        pl.semaphore_signal(barrier, inc=1, device_id=(v, s + 1, f), device_id_type=MESH)

    both = has_prev & has_next

    @pl.when(both)
    def _():
        pl.semaphore_wait(barrier, 4)

    @pl.when(~both)
    def _():
        pl.semaphore_wait(barrier, 3)

    def send_outer(k):
        def go(lo, n):
            c_y(k, lo, n).start()

            @pl.when(sends_halo & (k < AHEAD))
            def _():
                c_halo_own(k, lo, n).start()

        @pl.when(outer)
        def _():
            on(k, go)

    def send_inner(k):
        @pl.when(inner)
        def _():
            on(k, lambda lo, n: c_y(k, lo, n).start())

    def send_chip(k):
        def go(lo, n):
            c_core(k, lo, n).start()
            c_local(k, lo, n).start()

        on(k, go)

    def relay(k):
        def go(lo, n):
            arrived(across + 1, k, lo, n)
            c_fwd(k, lo, n).start()

            @pl.when(inner & sends_halo)
            def _():
                c_halo_fwd(k, lo, n).start()

        on(k, go)

    def relay_halo(k):
        def go(lo, n):
            arrived(halo_in, k, lo, n)
            c_halo_mate(k, lo, n).start()

        @pl.when(takes_halo)
        def _():
            on(k, go)

    def complete(k):
        def go(lo, n):
            c_local(k, lo, n).wait()
            arrived(mate + 1, k, lo, n)
            arrived(diag + 1, k, lo, n)

            @pl.when(sends_halo)
            def _():
                arrived(mate_slot, k, lo, n)

        on(k, go)

    @pl.loop(0, last + 1)
    def _(k):
        send_outer(k)
        send_chip(k)

    zero_row = jnp.zeros((cols, chans), x.dtype)
    for z in range(depth + 2):
        x[z, 0] = zero_row
        x[z, rows + 1] = zero_row

    def clear(z):
        @pl.loop(1, rows + 1)
        def _(r):
            x[z, r] = zero_row

    @pl.when(~has_prev)
    def _():
        clear(0)

    @pl.when(~has_next)
    def _():
        clear(depth + 1)

    get_w.wait()
    get_b.wait()
    for t in range(9):
        left, middle, right = (w_ref[3 * t + i] for i in range(3))
        tap = jnp.concatenate([middle, left, right, jnp.zeros_like(left)], axis=0)
        matrix[chans * t : chans * (t + 1)] = tap.T

    bias = b_ref[...].astype(jnp.float32)
    lead = jnp.where(inner, LEAD, 0)

    @pl.loop(0, last + 2 + LEAD)
    def _(step):
        t = step - LEAD
        relay(t + lead)

        @pl.when(inner & (t == 0))
        def _():
            @pl.loop(0, last + 1)
            def _(k):
                send_inner(k)

        @pl.when(outer & sends_halo & (t >= 0))
        def _():
            k = t + AHEAD
            on(k, lambda lo, n: c_halo_own(k, lo, n).start())

        relay_halo(t)
        complete(t - 1)

        @pl.when((t >= 2) & (t < last - TAIL + 2))
        def _():
            out_ref[:, pl.ds(2 * (t - 2), 2)] = convolve(x, matrix, bias, t - 2, depth)

    whole = (0, rows)
    c_y(0, *whole).wait_send()
    c_core(0, *whole).wait_send()
    c_fwd(0, *whole).wait_send()

    @pl.when(sends_halo)
    def _():
        c_halo_own(0, *whole).wait_send()

    @pl.when(takes_halo)
    def _():
        c_halo_mate(0, *whole).wait_send()


def finish(done, x, matrix, b_ref, result, tail, sems):
    depth, rows = result.shape[:2]
    first = done.shape[1]
    half = first // 2
    copies = []
    for z in range(depth):
        for i in range(2):
            part = pl.ds(half * i, half)
            copies.append(pltpu.make_async_copy(done.at[z, part], result.at[z, part], sems.at[2 * z + i]))
    for copy in copies:
        copy.start()
    bias = b_ref[...].astype(jnp.float32)
    for i in range(TAIL):
        tail[:, 2 * i : 2 * i + 2] = convolve(x, matrix, bias, first // 2 + i, depth)
        copies.append(
            pltpu.make_async_copy(
                tail.at[:, pl.ds(2 * i, 2)], result.at[:, pl.ds(first + 2 * i, 2)], sems.at[2 * depth + i]
            )
        )
        copies[-1].start()
    for copy in copies:
        copy.wait()


def body(volume, weights, bias):
    planes, rows, cols, chans = volume.shape
    outs = weights.shape[0]
    slabs = lax.axis_size("slab")
    depth = planes * lax.axis_size("filt")
    chunks = rows // 2 + 1
    taps = weights.transpose(1, 0, 2)
    early = rows - 2 * TAIL
    flops = 2 * depth * cols * outs * 27 * chans
    done, x, matrix, b = pl.pallas_call(
        functools.partial(kernel, slabs),
        out_shape=[
            pltpu.VMEM((depth, early, cols, outs), jnp.bfloat16),
            pltpu.VMEM((depth + 2, rows + 2, cols, chans), jnp.bfloat16),
            pltpu.VMEM((9 * chans, 4 * outs), jnp.bfloat16),
            pltpu.VMEM((1, outs), jnp.bfloat16),
        ],
        in_specs=[pl.BlockSpec(memory_space=pltpu.HBM)] * 3,
        out_specs=[pl.BlockSpec(memory_space=pltpu.VMEM)] * 4,
        scratch_shapes=[
            pltpu.VMEM(taps.shape, jnp.bfloat16),
            pltpu.SemaphoreType.DMA((5,)),
            pltpu.SemaphoreType.DMA((6, chunks)),
            pltpu.SemaphoreType.DMA((chunks,)),
            pltpu.SemaphoreType.DMA((2,)),
        ],
        compiler_params=pltpu.CompilerParams(
            collective_id=0, has_side_effects=True, vmem_limit_bytes=44 * 1024 * 1024
        ),
        cost_estimate=pl.CostEstimate(
            flops=flops * early, bytes_accessed=16 * rows * cols * chans, transcendentals=0
        ),
    )(volume, taps, bias.reshape(1, outs))
    return pl.pallas_call(
        finish,
        out_shape=jax.ShapeDtypeStruct((depth, rows, cols, outs), jnp.bfloat16),
        in_specs=[pl.BlockSpec(memory_space=pltpu.VMEM)] * 4,
        out_specs=pl.BlockSpec(memory_space=pltpu.HBM),
        scratch_shapes=[
            pltpu.VMEM((depth, 2 * TAIL, cols, outs), jnp.bfloat16),
            pltpu.SemaphoreType.DMA((2 * depth + TAIL,)),
        ],
        compiler_params=pltpu.CompilerParams(vmem_limit_bytes=16 * 1024 * 1024),
        cost_estimate=pl.CostEstimate(
            flops=flops * 2 * TAIL, bytes_accessed=4 * depth * rows * cols * outs, transcendentals=0
        ),
    )(done, x, matrix, b)


def solution(mesh):
    return jax.shard_map(
        body,
        mesh=mesh,
        in_specs=(P(("vol", "slab", "filt"), None, None, None), P("filt", None, None), P("filt")),
        out_specs=P(("vol", "slab"), None, None, "filt"),
        check_vma=False,
    )
```

```python
import functools

import jax
import jax.numpy as jnp
from jax import lax
from jax.experimental import pallas as pl
from jax.experimental.pallas import tpu as pltpu
from jax.sharding import PartitionSpec as P

MESH = pl.DeviceIdType.MESH
ROWS = 2
LEAD = 6
TAIL = 2
Y, HALO, CHIP = range(3)


def convolve(x, matrix, bias, k, depth):
    cols, chans = x.shape[2:]
    outs = bias.shape[-1]
    m = depth * ROWS * cols
    windows = [
        x[pl.ds(dz, depth), pl.ds(ROWS * k + dy, ROWS)].reshape(m, chans) for dz in range(3) for dy in range(3)
    ]
    total = jnp.dot(jnp.concatenate(windows, axis=1), matrix[...], preferred_element_type=jnp.float32)
    place = lax.rem(lax.broadcasted_iota(jnp.int32, (m, 2 * outs), 0), cols)
    near = total[:, : 2 * outs]
    far = total[:, 2 * outs :]
    before = jnp.where(place == 0, 0.0, pltpu.roll(near, 1, 0))
    after = jnp.where(place == cols - 1, 0.0, pltpu.roll(far, m - 1, 0))
    full = near + after + pltpu.roll(before, outs, 1)
    shifted = full[:, :outs] + bias
    result = jnp.where(shifted > 0, shifted, 0.3 * shifted)
    return result.astype(jnp.bfloat16).reshape(depth, ROWS, cols, outs)


def kernel(slabs, vol_ref, w_hbm, b_hbm, out_ref, x, matrix, b_ref, w_ref, send, recv, params):
    rows, cols, chans = vol_ref.shape[1:]
    depth = out_ref.shape[0]
    chunks = rows // ROWS
    v = lax.axis_index("vol")
    s = lax.axis_index("slab")
    f = lax.axis_index("filt")
    odd = lax.rem(f, 2)
    mate = f + 1 - 2 * odd
    across = lax.rem(f + 2, 4)
    outer = (f == 0) | (f == 3)
    inner = ~outer
    has_prev = s > 0
    has_next = s < slabs - 1
    is_odd = odd == 1
    halo_to = s + 2 * odd - 1
    halo_in = 5 - 5 * odd
    sends_halo = (is_odd & has_next) | (~is_odd & has_prev)
    takes_halo = (is_odd & has_prev) | (~is_odd & has_next)

    to_across = (v, s, across)
    to_mate = (v, s, mate)
    to_halo = (v, halo_to, f)

    def own(k):
        return vol_ref.at[0, pl.ds(ROWS * k, ROWS)]

    def slot(z, k):
        return x.at[z, pl.ds(ROWS * k + 1, ROWS)]

    def remote(src, z, k, kind, stream, dev):
        return pltpu.make_async_remote_copy(
            src_ref=src,
            dst_ref=slot(z, k),
            send_sem=send.at[kind],
            recv_sem=recv.at[stream, k],
            device_id=dev,
            device_id_type=MESH,
        )

    def c_y(k):
        return remote(own(k), f + 1, k, 0, Y, to_across)

    def c_core(k):
        return remote(own(k), f + 1, k, 1, CHIP, to_mate)

    def c_fwd(k):
        return remote(slot(across + 1, k), across + 1, k, 2, CHIP, to_mate)

    def c_halo_own(k):
        return remote(own(k), halo_in, k, 3, HALO, to_halo)

    def c_halo_fwd(k):
        return remote(slot(across + 1, k), halo_in, k, 3, HALO, to_halo)

    def c_halo_mate(k):
        return remote(slot(halo_in, k), halo_in, k, 4, CHIP, to_mate)

    def c_local(k):
        return pltpu.make_async_copy(own(k), slot(f + 1, k), recv.at[CHIP, k])

    def landed(ref, send_sem, recv_sem):
        return pltpu.make_async_remote_copy(
            src_ref=ref, dst_ref=ref, send_sem=send_sem, recv_sem=recv_sem, device_id=to_mate, device_id_type=MESH
        )

    def arrived(stream, planes, k):
        part = x.at[pl.ds(0, planes), pl.ds(ROWS * k + 1, ROWS)]
        landed(part, send.at[0], recv.at[stream, k]).wait_recv()

    def sent(kind):
        landed(x.at[0, pl.ds(1, rows)], send.at[kind], recv.at[Y, 0]).wait_send()

    get_w = pltpu.make_async_copy(w_hbm, w_ref, params.at[0])
    get_b = pltpu.make_async_copy(b_hbm, b_ref, params.at[1])
    get_w.start()
    get_b.start()

    barrier = pltpu.get_barrier_semaphore()
    pl.semaphore_signal(barrier, inc=1, device_id=to_mate, device_id_type=MESH)
    pl.semaphore_signal(barrier, inc=1, device_id=to_across, device_id_type=MESH)

    @pl.when(has_prev)
    def _():
        pl.semaphore_signal(barrier, inc=1, device_id=(v, s - 1, f), device_id_type=MESH)

    @pl.when(has_next)
    def _():
        pl.semaphore_signal(barrier, inc=1, device_id=(v, s + 1, f), device_id_type=MESH)

    greeted = 2 + has_prev.astype(jnp.int32) + has_next.astype(jnp.int32)
    pl.semaphore_wait(barrier, greeted)

    @pl.loop(0, chunks)
    def _(k):
        @pl.when(outer)
        def _():
            c_y(k).start()

        @pl.when(outer & sends_halo & (k < LEAD))
        def _():
            c_halo_own(k).start()

        c_core(k).start()
        c_local(k).start()

    zero_row = jnp.zeros((cols, chans), x.dtype)
    for z in range(depth + 2):
        x[z, 0] = zero_row
        x[z, rows + 1] = zero_row

    def clear(z):
        @pl.loop(1, rows + 1)
        def _(r):
            x[z, r] = zero_row

    @pl.when(~has_prev)
    def _():
        clear(0)

    @pl.when(~has_next)
    def _():
        clear(depth + 1)

    def relay(k):
        arrived(Y, 1, k)
        c_fwd(k).start()

        @pl.when(inner & sends_halo)
        def _():
            c_halo_fwd(k).start()

    def relay_halo(k):
        @pl.when(takes_halo)
        def _():
            arrived(HALO, 1, k)
            c_halo_mate(k).start()

    def complete(k):
        @pl.when(sends_halo)
        def _():
            arrived(CHIP, 4, k)

        @pl.when(~sends_halo)
        def _():
            arrived(CHIP, 3, k)

    @pl.when(inner)
    def _():
        @pl.loop(0, LEAD)
        def _(k):
            relay(k)

        @pl.loop(0, chunks)
        def _(k):
            c_y(k).start()

    get_w.wait()
    get_b.wait()
    for t in range(9):
        left, middle, right = (w_ref[3 * t + i] for i in range(3))
        tap = jnp.concatenate([middle, left, right, jnp.zeros_like(left)], axis=0)
        matrix[chans * t : chans * (t + 1)] = tap.T

    bias = b_ref[...].astype(jnp.float32)
    lead = jnp.where(inner, LEAD, 0)

    @pl.loop(0, chunks)
    def _(t):
        @pl.when(t + lead < chunks)
        def _():
            relay(t + lead)

        @pl.when(outer & sends_halo & (t + LEAD < chunks))
        def _():
            c_halo_own(t + LEAD).start()

        relay_halo(t)

        @pl.when(t >= 1)
        def _():
            complete(t - 1)

        @pl.when((t >= 2) & (t < chunks - TAIL + 2))
        def _():
            out_ref[:, pl.ds(ROWS * (t - 2), ROWS)] = convolve(x, matrix, bias, t - 2, depth)

    complete(chunks - 1)
    for kind in range(3):
        sent(kind)

    @pl.when(sends_halo)
    def _():
        sent(3)

    @pl.when(takes_halo)
    def _():
        sent(4)


def finish(done, x, matrix, b_ref, result, tail, sems):
    depth, first, cols, outs = done.shape
    copies = [pltpu.make_async_copy(done.at[z], result.at[z, pl.ds(0, first)], sems.at[z]) for z in range(depth)]
    for copy in copies:
        copy.start()
    bias = b_ref[...].astype(jnp.float32)

    def put(i):
        return pltpu.make_async_copy(
            tail.at[:, pl.ds(ROWS * i, ROWS)],
            result.at[:, pl.ds(first + ROWS * i, ROWS)],
            sems.at[depth + i],
        )

    @pl.loop(0, TAIL)
    def _(i):
        tail[:, pl.ds(ROWS * i, ROWS)] = convolve(x, matrix, bias, first // ROWS + i, depth)
        put(i).start()

    for copy in copies:
        copy.wait()
    for i in range(TAIL):
        put(i).wait()


def body(volume, weights, bias):
    planes, rows, cols, chans = volume.shape
    outs = weights.shape[0]
    slabs = lax.axis_size("slab")
    depth = planes * lax.axis_size("filt")
    taps = weights.transpose(1, 0, 2)
    early = rows - ROWS * TAIL
    flops = 2 * depth * cols * outs * 27 * chans
    done, x, matrix, b = pl.pallas_call(
        functools.partial(kernel, slabs),
        out_shape=[
            pltpu.VMEM((depth, early, cols, outs), jnp.bfloat16),
            pltpu.VMEM((depth + 2, rows + 2, cols, chans), jnp.bfloat16),
            pltpu.VMEM((9 * chans, 4 * outs), jnp.bfloat16),
            pltpu.VMEM((1, outs), jnp.bfloat16),
        ],
        in_specs=[pl.BlockSpec(memory_space=pltpu.HBM)] * 3,
        out_specs=[pl.BlockSpec(memory_space=pltpu.VMEM)] * 4,
        scratch_shapes=[
            pltpu.VMEM(taps.shape, jnp.bfloat16),
            pltpu.SemaphoreType.DMA((5,)),
            pltpu.SemaphoreType.DMA((3, rows // ROWS)),
            pltpu.SemaphoreType.DMA((2,)),
        ],
        compiler_params=pltpu.CompilerParams(
            collective_id=0, has_side_effects=True, vmem_limit_bytes=44 * 1024 * 1024
        ),
        cost_estimate=pl.CostEstimate(
            flops=flops * early, bytes_accessed=16 * rows * cols * chans, transcendentals=0
        ),
    )(volume, taps, bias.reshape(1, outs))
    return pl.pallas_call(
        finish,
        out_shape=jax.ShapeDtypeStruct((depth, rows, cols, outs), jnp.bfloat16),
        in_specs=[pl.BlockSpec(memory_space=pltpu.VMEM)] * 4,
        out_specs=pl.BlockSpec(memory_space=pltpu.HBM),
        scratch_shapes=[
            pltpu.VMEM((depth, ROWS * TAIL, cols, outs), jnp.bfloat16),
            pltpu.SemaphoreType.DMA((depth + TAIL,)),
        ],
        compiler_params=pltpu.CompilerParams(vmem_limit_bytes=16 * 1024 * 1024),
        cost_estimate=pl.CostEstimate(
            flops=flops * ROWS * TAIL, bytes_accessed=4 * depth * rows * cols * outs, transcendentals=0
        ),
    )(done, x, matrix, b)


def solution(mesh):
    return jax.shard_map(
        body,
        mesh=mesh,
        in_specs=(P(("vol", "slab", "filt"), None, None, None), P("filt", None, None), P("filt")),
        out_specs=P(("vol", "slab"), None, None, "filt"),
        check_vma=False,
    )
```

```python
import functools

import jax
import jax.numpy as jnp
from jax import lax
from jax.experimental import pallas as pl
from jax.experimental.pallas import tpu as pltpu
from jax.sharding import PartitionSpec as P

MESH = pl.DeviceIdType.MESH
ROWS = 2
LEAD = 4
AHEAD = 9
TAIL = 2
Y, HALO, CHIP = range(3)


def convolve(x, matrix, bias, k, depth):
    cols, chans = x.shape[2:]
    outs = bias.shape[-1]
    m = depth * ROWS * cols
    windows = [
        x[pl.ds(dz, depth), pl.ds(ROWS * k + dy, ROWS)].reshape(m, chans) for dz in range(3) for dy in range(3)
    ]
    total = jnp.dot(jnp.concatenate(windows, axis=1), matrix[...], preferred_element_type=jnp.float32)
    place = lax.rem(lax.broadcasted_iota(jnp.int32, (m, 2 * outs), 0), cols)
    near = total[:, : 2 * outs]
    far = total[:, 2 * outs :]
    before = jnp.where(place == 0, 0.0, pltpu.roll(near, 1, 0))
    after = jnp.where(place == cols - 1, 0.0, pltpu.roll(far, m - 1, 0))
    full = near + after + pltpu.roll(before, outs, 1)
    shifted = full[:, :outs] + bias
    result = jnp.where(shifted > 0, shifted, 0.3 * shifted)
    return result.astype(jnp.bfloat16).reshape(depth, ROWS, cols, outs)


def kernel(slabs, vol_ref, w_hbm, b_hbm, out_ref, x, matrix, b_ref, w_ref, send, recv, params):
    rows, cols, chans = vol_ref.shape[1:]
    depth = out_ref.shape[0]
    chunks = rows // ROWS
    v = lax.axis_index("vol")
    s = lax.axis_index("slab")
    f = lax.axis_index("filt")
    odd = lax.rem(f, 2)
    mate = f + 1 - 2 * odd
    across = lax.rem(f + 2, 4)
    outer = (f == 0) | (f == 3)
    inner = ~outer
    has_prev = s > 0
    has_next = s < slabs - 1
    is_odd = odd == 1
    halo_to = s + 2 * odd - 1
    halo_in = 5 - 5 * odd
    sends_halo = (is_odd & has_next) | (~is_odd & has_prev)
    takes_halo = (is_odd & has_prev) | (~is_odd & has_next)

    to_across = (v, s, across)
    to_mate = (v, s, mate)
    to_halo = (v, halo_to, f)

    def own(k):
        return vol_ref.at[0, pl.ds(ROWS * k, ROWS)]

    def slot(z, k):
        return x.at[z, pl.ds(ROWS * k + 1, ROWS)]

    def remote(src, z, k, kind, stream, dev):
        return pltpu.make_async_remote_copy(
            src_ref=src,
            dst_ref=slot(z, k),
            send_sem=send.at[kind],
            recv_sem=recv.at[stream, k],
            device_id=dev,
            device_id_type=MESH,
        )

    def c_y(k):
        return remote(own(k), f + 1, k, 0, Y, to_across)

    def c_core(k):
        return remote(own(k), f + 1, k, 1, CHIP, to_mate)

    def c_fwd(k):
        return remote(slot(across + 1, k), across + 1, k, 2, CHIP, to_mate)

    def c_halo_own(k):
        return remote(own(k), halo_in, k, 3, HALO, to_halo)

    def c_halo_fwd(k):
        return remote(slot(across + 1, k), halo_in, k, 3, HALO, to_halo)

    def c_halo_mate(k):
        return remote(slot(halo_in, k), halo_in, k, 4, CHIP, to_mate)

    def c_local(k):
        return pltpu.make_async_copy(own(k), slot(f + 1, k), recv.at[CHIP, k])

    def landed(ref, send_sem, recv_sem):
        return pltpu.make_async_remote_copy(
            src_ref=ref, dst_ref=ref, send_sem=send_sem, recv_sem=recv_sem, device_id=to_mate, device_id_type=MESH
        )

    def arrived(stream, planes, k):
        part = x.at[pl.ds(0, planes), pl.ds(ROWS * k + 1, ROWS)]
        landed(part, send.at[0], recv.at[stream, k]).wait_recv()

    def sent(kind):
        landed(x.at[0, pl.ds(1, rows)], send.at[kind], recv.at[Y, 0]).wait_send()

    get_w = pltpu.make_async_copy(w_hbm, w_ref, params.at[0])
    get_b = pltpu.make_async_copy(b_hbm, b_ref, params.at[1])
    get_w.start()
    get_b.start()

    barrier = pltpu.get_barrier_semaphore()
    pl.semaphore_signal(barrier, inc=1, device_id=to_mate, device_id_type=MESH)
    pl.semaphore_signal(barrier, inc=1, device_id=to_across, device_id_type=MESH)

    @pl.when(has_prev)
    def _():
        pl.semaphore_signal(barrier, inc=1, device_id=(v, s - 1, f), device_id_type=MESH)

    @pl.when(has_next)
    def _():
        pl.semaphore_signal(barrier, inc=1, device_id=(v, s + 1, f), device_id_type=MESH)

    greeted = 2 + has_prev.astype(jnp.int32) + has_next.astype(jnp.int32)
    pl.semaphore_wait(barrier, greeted)

    @pl.loop(0, chunks)
    def _(k):
        @pl.when(outer)
        def _():
            c_y(k).start()

        @pl.when(outer & sends_halo & (k < AHEAD))
        def _():
            c_halo_own(k).start()

        c_core(k).start()
        c_local(k).start()

    zero_row = jnp.zeros((cols, chans), x.dtype)
    for z in range(depth + 2):
        x[z, 0] = zero_row
        x[z, rows + 1] = zero_row

    def clear(z):
        @pl.loop(1, rows + 1)
        def _(r):
            x[z, r] = zero_row

    @pl.when(~has_prev)
    def _():
        clear(0)

    @pl.when(~has_next)
    def _():
        clear(depth + 1)

    def relay(k):
        arrived(Y, 1, k)
        c_fwd(k).start()

        @pl.when(inner & sends_halo)
        def _():
            c_halo_fwd(k).start()

    def relay_halo(k):
        @pl.when(takes_halo)
        def _():
            arrived(HALO, 1, k)
            c_halo_mate(k).start()

    def complete(k):
        @pl.when(sends_halo)
        def _():
            arrived(CHIP, 4, k)

        @pl.when(~sends_halo)
        def _():
            arrived(CHIP, 3, k)

    @pl.when(inner)
    def _():
        @pl.loop(0, LEAD)
        def _(k):
            relay(k)

        @pl.loop(0, chunks)
        def _(k):
            c_y(k).start()

    get_w.wait()
    get_b.wait()
    for t in range(9):
        left, middle, right = (w_ref[3 * t + i] for i in range(3))
        tap = jnp.concatenate([middle, left, right, jnp.zeros_like(left)], axis=0)
        matrix[chans * t : chans * (t + 1)] = tap.T

    bias = b_ref[...].astype(jnp.float32)
    lead = jnp.where(inner, LEAD, 0)

    @pl.loop(0, chunks)
    def _(t):
        @pl.when(t + lead < chunks)
        def _():
            relay(t + lead)

        @pl.when(outer & sends_halo & (t + AHEAD < chunks))
        def _():
            c_halo_own(t + AHEAD).start()

        relay_halo(t)

        @pl.when(t >= 1)
        def _():
            complete(t - 1)

        @pl.when((t >= 2) & (t < chunks - TAIL + 2))
        def _():
            out_ref[:, pl.ds(ROWS * (t - 2), ROWS)] = convolve(x, matrix, bias, t - 2, depth)

    complete(chunks - 1)
    for kind in range(3):
        sent(kind)

    @pl.when(sends_halo)
    def _():
        sent(3)

    @pl.when(takes_halo)
    def _():
        sent(4)


def finish(done, x, matrix, b_ref, result, tail, sems):
    depth, first, cols, outs = done.shape
    copies = [pltpu.make_async_copy(done.at[z], result.at[z, pl.ds(0, first)], sems.at[z]) for z in range(depth)]
    for copy in copies:
        copy.start()
    bias = b_ref[...].astype(jnp.float32)

    def put(i):
        return pltpu.make_async_copy(
            tail.at[:, pl.ds(ROWS * i, ROWS)],
            result.at[:, pl.ds(first + ROWS * i, ROWS)],
            sems.at[depth + i],
        )

    @pl.loop(0, TAIL)
    def _(i):
        tail[:, pl.ds(ROWS * i, ROWS)] = convolve(x, matrix, bias, first // ROWS + i, depth)
        put(i).start()

    for copy in copies:
        copy.wait()
    for i in range(TAIL):
        put(i).wait()


def body(volume, weights, bias):
    planes, rows, cols, chans = volume.shape
    outs = weights.shape[0]
    slabs = lax.axis_size("slab")
    depth = planes * lax.axis_size("filt")
    taps = weights.transpose(1, 0, 2)
    early = rows - ROWS * TAIL
    flops = 2 * depth * cols * outs * 27 * chans
    done, x, matrix, b = pl.pallas_call(
        functools.partial(kernel, slabs),
        out_shape=[
            pltpu.VMEM((depth, early, cols, outs), jnp.bfloat16),
            pltpu.VMEM((depth + 2, rows + 2, cols, chans), jnp.bfloat16),
            pltpu.VMEM((9 * chans, 4 * outs), jnp.bfloat16),
            pltpu.VMEM((1, outs), jnp.bfloat16),
        ],
        in_specs=[pl.BlockSpec(memory_space=pltpu.HBM)] * 3,
        out_specs=[pl.BlockSpec(memory_space=pltpu.VMEM)] * 4,
        scratch_shapes=[
            pltpu.VMEM(taps.shape, jnp.bfloat16),
            pltpu.SemaphoreType.DMA((5,)),
            pltpu.SemaphoreType.DMA((3, rows // ROWS)),
            pltpu.SemaphoreType.DMA((2,)),
        ],
        compiler_params=pltpu.CompilerParams(
            collective_id=0, has_side_effects=True, vmem_limit_bytes=44 * 1024 * 1024
        ),
        cost_estimate=pl.CostEstimate(
            flops=flops * early, bytes_accessed=16 * rows * cols * chans, transcendentals=0
        ),
    )(volume, taps, bias.reshape(1, outs))
    return pl.pallas_call(
        finish,
        out_shape=jax.ShapeDtypeStruct((depth, rows, cols, outs), jnp.bfloat16),
        in_specs=[pl.BlockSpec(memory_space=pltpu.VMEM)] * 4,
        out_specs=pl.BlockSpec(memory_space=pltpu.HBM),
        scratch_shapes=[
            pltpu.VMEM((depth, ROWS * TAIL, cols, outs), jnp.bfloat16),
            pltpu.SemaphoreType.DMA((depth + TAIL,)),
        ],
        compiler_params=pltpu.CompilerParams(vmem_limit_bytes=16 * 1024 * 1024),
        cost_estimate=pl.CostEstimate(
            flops=flops * ROWS * TAIL, bytes_accessed=4 * depth * rows * cols * outs, transcendentals=0
        ),
    )(done, x, matrix, b)


def solution(mesh):
    return jax.shard_map(
        body,
        mesh=mesh,
        in_specs=(P(("vol", "slab", "filt"), None, None, None), P("filt", None, None), P("filt")),
        out_specs=P(("vol", "slab"), None, None, "filt"),
        check_vma=False,
    )
```

```python
import functools

import jax
import jax.numpy as jnp
from jax import lax
from jax.experimental import pallas as pl
from jax.experimental.pallas import tpu as pltpu
from jax.sharding import PartitionSpec as P

MESH = pl.DeviceIdType.MESH
ROWS = 2
LEAD = 4
AHEAD = 9
TAIL = 2
PIECES = 4


def convolve(x, matrix, bias, row, rows, depth):
    cols, chans = x.shape[2:]
    outs = bias.shape[-1]
    m = depth * rows * cols
    windows = [x[pl.ds(dz, depth), pl.ds(row + dy, rows)].reshape(m, chans) for dz in range(3) for dy in range(3)]
    total = jnp.dot(jnp.concatenate(windows, axis=1), matrix[...], preferred_element_type=jnp.float32)
    place = lax.rem(lax.broadcasted_iota(jnp.int32, (m, 2 * outs), 0), cols)
    near = total[:, : 2 * outs]
    far = total[:, 2 * outs :]
    before = jnp.where(place == 0, 0.0, pltpu.roll(near, 1, 0))
    after = jnp.where(place == cols - 1, 0.0, pltpu.roll(far, m - 1, 0))
    full = near + after + pltpu.roll(before, outs, 1)
    shifted = full[:, :outs] + bias
    result = jnp.where(shifted > 0, shifted, 0.3 * shifted)
    return result.astype(jnp.bfloat16).reshape(depth, rows, cols, outs)


def kernel(slabs, vol_ref, w_hbm, b_hbm, out_ref, x, matrix, b_ref, w_ref, send, over_y, met, params, spread):
    rows, cols, chans = vol_ref.shape[1:]
    depth = out_ref.shape[0]
    chunks = rows // ROWS
    v = lax.axis_index("vol")
    s = lax.axis_index("slab")
    f = lax.axis_index("filt")
    odd = lax.rem(f, 2)
    mate = f + 1 - 2 * odd
    across = lax.rem(f + 2, 4)
    outer = (f == 0) | (f == 3)
    inner = ~outer
    has_prev = s > 0
    has_next = s < slabs - 1
    is_odd = odd == 1
    halo_to = s + 2 * odd - 1
    halo_in = 5 - 5 * odd
    sends_halo = (is_odd & has_next) | (~is_odd & has_prev)
    takes_halo = (is_odd & has_prev) | (~is_odd & has_next)

    to_across = (v, s, across)
    to_mate = (v, s, mate)
    to_halo = (v, halo_to, f)

    def own(k):
        return vol_ref.at[0, pl.ds(ROWS * k, ROWS)]

    def slot(z, k):
        return x.at[z, pl.ds(ROWS * k + 1, ROWS)]

    def remote(src, z, k, kind, sem, dev):
        return pltpu.make_async_remote_copy(
            src_ref=src,
            dst_ref=slot(z, k),
            send_sem=send.at[kind],
            recv_sem=sem,
            device_id=dev,
            device_id_type=MESH,
        )

    def c_y(k):
        return remote(own(k), f + 1, k, 0, over_y.at[k], to_across)

    def c_fwd(k):
        return remote(slot(across + 1, k), across + 1, k, 2, met.at[k + 1], to_mate)

    def c_halo_own(k):
        return remote(own(k), halo_in, k, 3, met.at[k], to_halo)

    def c_halo_fwd(k):
        return remote(slot(across + 1, k), halo_in, k, 3, met.at[k], to_halo)

    def c_halo_mate(k):
        return remote(slot(halo_in, k), halo_in, k, 4, met.at[k + 1], to_mate)

    piece = rows // PIECES

    def c_local(i):
        part = pl.ds(piece * i, piece)
        return pltpu.make_async_copy(
            vol_ref.at[0, part], x.at[f + 1, pl.ds(piece * i + 1, piece)], spread.at[i]
        )

    def c_core(i):
        part = pl.ds(piece * i, piece)
        return pltpu.make_async_remote_copy(
            src_ref=vol_ref.at[0, part],
            dst_ref=x.at[f + 1, pl.ds(piece * i + 1, piece)],
            send_sem=send.at[1],
            recv_sem=spread.at[i],
            device_id=to_mate,
            device_id_type=MESH,
        )

    def landed(ref, send_sem, recv_sem):
        return pltpu.make_async_remote_copy(
            src_ref=ref, dst_ref=ref, send_sem=send_sem, recv_sem=recv_sem, device_id=to_mate, device_id_type=MESH
        )

    def arrived(sem, planes):
        part = x.at[pl.ds(0, planes), pl.ds(1, ROWS)]
        landed(part, send.at[0], sem).wait_recv()

    def sent(kind):
        landed(x.at[0, pl.ds(1, rows)], send.at[kind], over_y.at[0]).wait_send()

    get_w = pltpu.make_async_copy(w_hbm, w_ref, params.at[0])
    get_b = pltpu.make_async_copy(b_hbm, b_ref, params.at[1])
    get_w.start()
    get_b.start()

    barrier = pltpu.get_barrier_semaphore()
    pl.semaphore_signal(barrier, inc=1, device_id=to_mate, device_id_type=MESH)
    pl.semaphore_signal(barrier, inc=1, device_id=to_across, device_id_type=MESH)

    @pl.when(has_prev)
    def _():
        pl.semaphore_signal(barrier, inc=1, device_id=(v, s - 1, f), device_id_type=MESH)

    @pl.when(has_next)
    def _():
        pl.semaphore_signal(barrier, inc=1, device_id=(v, s + 1, f), device_id_type=MESH)

    greeted = 2 + has_prev.astype(jnp.int32) + has_next.astype(jnp.int32)
    pl.semaphore_wait(barrier, greeted)

    @pl.when(outer)
    def _():
        @pl.loop(0, chunks)
        def _(k):
            c_y(k).start()

            @pl.when(sends_halo & (k < AHEAD))
            def _():
                c_halo_own(k).start()

            @pl.when(k == 1)
            def _():
                for i in range(PIECES):
                    c_core(i).start()
                    c_local(i).start()

    @pl.when(inner)
    def _():
        for i in range(PIECES):
            c_core(i).start()
            c_local(i).start()

    zero_row = jnp.zeros((cols, chans), x.dtype)
    for z in range(depth + 2):
        x[z, 0] = zero_row
        x[z, rows + 1] = zero_row

    def clear(z):
        @pl.loop(1, rows + 1)
        def _(r):
            x[z, r] = zero_row

    @pl.when(~has_prev)
    def _():
        clear(0)

    @pl.when(~has_next)
    def _():
        clear(depth + 1)

    def relay(k):
        arrived(over_y.at[k], 1)
        c_fwd(k).start()

        @pl.when(inner & sends_halo)
        def _():
            c_halo_fwd(k).start()

    def meet(k):
        @pl.when(has_prev & has_next)
        def _():
            arrived(met.at[k], 3)

        @pl.when(~(has_prev & has_next))
        def _():
            arrived(met.at[k], 2)

    def pass_halo(k):
        @pl.when(takes_halo)
        def _():
            c_halo_mate(k).start()

    def spread_in(i):
        part = x.at[pl.ds(0, 2), pl.ds(piece * i + 1, piece)]
        landed(part, send.at[0], spread.at[i]).wait_recv()

    @pl.when(inner)
    def _():
        @pl.loop(0, LEAD)
        def _(k):
            relay(k)

        @pl.loop(0, chunks)
        def _(k):
            c_y(k).start()

    get_w.wait()
    get_b.wait()
    for t in range(9):
        left, middle, right = (w_ref[3 * t + i] for i in range(3))
        tap = jnp.concatenate([middle, left, right, jnp.zeros_like(left)], axis=0)
        matrix[chans * t : chans * (t + 1)] = tap.T

    bias = b_ref[...].astype(jnp.float32)
    lead = jnp.where(inner, LEAD, 0)

    @pl.loop(0, chunks)
    def _(t):
        @pl.when(t + lead < chunks)
        def _():
            relay(t + lead)

        @pl.when(outer & sends_halo & (t + AHEAD < chunks))
        def _():
            c_halo_own(t + AHEAD).start()

        @pl.when(t >= 1)
        def _():
            meet(t)

        @pl.when((t == 0) & takes_halo)
        def _():
            arrived(met.at[0], 1)

        pass_halo(t)

        @pl.when(lax.rem(t - 1, chunks // PIECES) == 0)
        def _():
            spread_in((t - 1) // (chunks // PIECES))

        @pl.when((t >= 2) & (t < chunks - TAIL + 2))
        def _():
            out_ref[:, pl.ds(ROWS * (t - 2), ROWS)] = convolve(x, matrix, bias, ROWS * (t - 2), ROWS, depth)

    @pl.when(sends_halo)
    def _():
        arrived(met.at[chunks], 2)

    @pl.when(~sends_halo)
    def _():
        arrived(met.at[chunks], 1)

    for kind in range(3):
        sent(kind)

    @pl.when(sends_halo)
    def _():
        sent(3)

    @pl.when(takes_halo)
    def _():
        sent(4)


def finish(done, x, matrix, b_ref, result, tail, sems):
    depth, first, cols, outs = done.shape
    copies = [pltpu.make_async_copy(done.at[z], result.at[z, pl.ds(0, first)], sems.at[z]) for z in range(depth)]
    for copy in copies:
        copy.start()
    bias = b_ref[...].astype(jnp.float32)

    tail[...] = convolve(x, matrix, bias, first, ROWS * TAIL, depth)
    put = pltpu.make_async_copy(tail, result.at[:, pl.ds(first, ROWS * TAIL)], sems.at[depth])
    put.start()
    for copy in copies + [put]:
        copy.wait()


def body(volume, weights, bias):
    planes, rows, cols, chans = volume.shape
    outs = weights.shape[0]
    slabs = lax.axis_size("slab")
    depth = planes * lax.axis_size("filt")
    taps = weights.transpose(1, 0, 2)
    early = rows - ROWS * TAIL
    flops = 2 * depth * cols * outs * 27 * chans
    done, x, matrix, b = pl.pallas_call(
        functools.partial(kernel, slabs),
        out_shape=[
            pltpu.VMEM((depth, early, cols, outs), jnp.bfloat16),
            pltpu.VMEM((depth + 2, rows + 2, cols, chans), jnp.bfloat16),
            pltpu.VMEM((9 * chans, 4 * outs), jnp.bfloat16),
            pltpu.VMEM((1, outs), jnp.bfloat16),
        ],
        in_specs=[pl.BlockSpec(memory_space=pltpu.HBM)] * 3,
        out_specs=[pl.BlockSpec(memory_space=pltpu.VMEM)] * 4,
        scratch_shapes=[
            pltpu.VMEM(taps.shape, jnp.bfloat16),
            pltpu.SemaphoreType.DMA((5,)),
            pltpu.SemaphoreType.DMA((rows // ROWS,)),
            pltpu.SemaphoreType.DMA((rows // ROWS + 1,)),
            pltpu.SemaphoreType.DMA((2,)),
            pltpu.SemaphoreType.DMA((PIECES,)),
        ],
        compiler_params=pltpu.CompilerParams(
            collective_id=0, has_side_effects=True, vmem_limit_bytes=44 * 1024 * 1024
        ),
        cost_estimate=pl.CostEstimate(
            flops=flops * early, bytes_accessed=16 * rows * cols * chans, transcendentals=0
        ),
    )(volume, taps, bias.reshape(1, outs))
    return pl.pallas_call(
        finish,
        out_shape=jax.ShapeDtypeStruct((depth, rows, cols, outs), jnp.bfloat16),
        in_specs=[pl.BlockSpec(memory_space=pltpu.VMEM)] * 4,
        out_specs=pl.BlockSpec(memory_space=pltpu.HBM),
        scratch_shapes=[
            pltpu.VMEM((depth, ROWS * TAIL, cols, outs), jnp.bfloat16),
            pltpu.SemaphoreType.DMA((depth + 1,)),
        ],
        compiler_params=pltpu.CompilerParams(vmem_limit_bytes=16 * 1024 * 1024),
        cost_estimate=pl.CostEstimate(
            flops=flops * ROWS * TAIL, bytes_accessed=4 * depth * rows * cols * outs, transcendentals=0
        ),
    )(done, x, matrix, b)


def solution(mesh):
    return jax.shard_map(
        body,
        mesh=mesh,
        in_specs=(P(("vol", "slab", "filt"), None, None, None), P("filt", None, None), P("filt")),
        out_specs=P(("vol", "slab"), None, None, "filt"),
        check_vma=False,
    )
```

```python
import functools

import jax
import jax.numpy as jnp
from jax import lax
from jax.experimental import pallas as pl
from jax.experimental.pallas import tpu as pltpu
from jax.sharding import PartitionSpec as P

MESH = pl.DeviceIdType.MESH
ROWS = 2
LEAD = 4
AHEAD = 9
TAIL = 2
PIECES = 4


def convolve(x, matrix, bias, row, rows, depth):
    cols, chans = x.shape[2:]
    outs = bias.shape[-1]
    m = depth * rows * cols
    windows = [x[pl.ds(dz, depth), pl.ds(row + dy, rows)].reshape(m, chans) for dz in range(3) for dy in range(3)]
    total = jnp.dot(jnp.concatenate(windows, axis=1), matrix[...], preferred_element_type=jnp.float32)
    place = lax.rem(lax.broadcasted_iota(jnp.int32, (m, 2 * outs), 0), cols)
    near = total[:, : 2 * outs]
    far = total[:, 2 * outs :]
    before = jnp.where(place == 0, 0.0, pltpu.roll(near, 1, 0))
    after = jnp.where(place == cols - 1, 0.0, pltpu.roll(far, m - 1, 0))
    full = near + after + pltpu.roll(before, outs, 1)
    shifted = full[:, :outs] + bias
    result = jnp.where(shifted > 0, shifted, 0.3 * shifted)
    return result.astype(jnp.bfloat16).reshape(depth, rows, cols, outs)


def kernel(slabs, vol_ref, w_hbm, b_hbm, out_ref, x, matrix, b_ref, w_ref, send, over_y, met, params, spread):
    rows, cols, chans = vol_ref.shape[1:]
    depth = out_ref.shape[0]
    chunks = rows // ROWS
    v = lax.axis_index("vol")
    s = lax.axis_index("slab")
    f = lax.axis_index("filt")
    odd = lax.rem(f, 2)
    mate = f + 1 - 2 * odd
    across = lax.rem(f + 2, 4)
    outer = (f == 0) | (f == 3)
    inner = ~outer
    has_prev = s > 0
    has_next = s < slabs - 1
    is_odd = odd == 1
    halo_to = s + 2 * odd - 1
    halo_in = 5 - 5 * odd
    sends_halo = (is_odd & has_next) | (~is_odd & has_prev)
    takes_halo = (is_odd & has_prev) | (~is_odd & has_next)

    to_across = (v, s, across)
    to_mate = (v, s, mate)
    to_halo = (v, halo_to, f)

    def own(k):
        return vol_ref.at[0, pl.ds(ROWS * k, ROWS)]

    def slot(z, k):
        return x.at[z, pl.ds(ROWS * k + 1, ROWS)]

    def remote(src, z, k, kind, sem, dev):
        return pltpu.make_async_remote_copy(
            src_ref=src,
            dst_ref=slot(z, k),
            send_sem=send.at[kind],
            recv_sem=sem,
            device_id=dev,
            device_id_type=MESH,
        )

    def c_y(k):
        return remote(own(k), f + 1, k, 0, over_y.at[k], to_across)

    def c_fwd(k):
        return remote(slot(across + 1, k), across + 1, k, 2, met.at[k + 1], to_mate)

    def c_halo_own(k):
        return remote(own(k), halo_in, k, 3, met.at[k], to_halo)

    def c_halo_fwd(k):
        return remote(slot(across + 1, k), halo_in, k, 3, met.at[k], to_halo)

    def c_halo_mate(k):
        return remote(slot(halo_in, k), halo_in, k, 4, met.at[k + 1], to_mate)

    piece = rows // PIECES

    def c_local(i):
        part = pl.ds(piece * i, piece)
        return pltpu.make_async_copy(
            vol_ref.at[0, part], x.at[f + 1, pl.ds(piece * i + 1, piece)], spread.at[i]
        )

    def c_core(i):
        part = pl.ds(piece * i, piece)
        return pltpu.make_async_remote_copy(
            src_ref=vol_ref.at[0, part],
            dst_ref=x.at[f + 1, pl.ds(piece * i + 1, piece)],
            send_sem=send.at[1],
            recv_sem=spread.at[i],
            device_id=to_mate,
            device_id_type=MESH,
        )

    def landed(ref, send_sem, recv_sem):
        return pltpu.make_async_remote_copy(
            src_ref=ref, dst_ref=ref, send_sem=send_sem, recv_sem=recv_sem, device_id=to_mate, device_id_type=MESH
        )

    def arrived(sem, planes):
        part = x.at[pl.ds(0, planes), pl.ds(1, ROWS)]
        landed(part, send.at[0], sem).wait_recv()

    def sent(kind):
        landed(x.at[0, pl.ds(1, rows)], send.at[kind], over_y.at[0]).wait_send()

    get_w = pltpu.make_async_copy(w_hbm, w_ref, params.at[0])
    get_b = pltpu.make_async_copy(b_hbm, b_ref, params.at[1])
    get_w.start()
    get_b.start()

    barrier = pltpu.get_barrier_semaphore()
    pl.semaphore_signal(barrier, inc=1, device_id=to_mate, device_id_type=MESH)
    pl.semaphore_signal(barrier, inc=1, device_id=to_across, device_id_type=MESH)

    @pl.when(has_prev)
    def _():
        pl.semaphore_signal(barrier, inc=1, device_id=(v, s - 1, f), device_id_type=MESH)

    @pl.when(has_next)
    def _():
        pl.semaphore_signal(barrier, inc=1, device_id=(v, s + 1, f), device_id_type=MESH)

    greeted = 2 + has_prev.astype(jnp.int32) + has_next.astype(jnp.int32)
    pl.semaphore_wait(barrier, greeted)

    @pl.when(outer)
    def _():
        @pl.loop(0, chunks)
        def _(k):
            c_y(k).start()

            @pl.when(sends_halo & (k < AHEAD))
            def _():
                c_halo_own(k).start()

            @pl.when(k == 1)
            def _():
                for i in range(PIECES):
                    c_core(i).start()
                    c_local(i).start()

    @pl.when(inner)
    def _():
        for i in range(PIECES):
            c_core(i).start()
            c_local(i).start()

    zero_row = jnp.zeros((cols, chans), x.dtype)
    for z in range(depth + 2):
        x[z, 0] = zero_row
        x[z, rows + 1] = zero_row

    def clear(z):
        @pl.loop(1, rows + 1)
        def _(r):
            x[z, r] = zero_row

    @pl.when(~has_prev)
    def _():
        clear(0)

    @pl.when(~has_next)
    def _():
        clear(depth + 1)

    def relay(k):
        arrived(over_y.at[k], 1)
        c_fwd(k).start()

        @pl.when(inner & sends_halo)
        def _():
            c_halo_fwd(k).start()

    def meet(k):
        @pl.when(has_prev & has_next)
        def _():
            arrived(met.at[k], 3)

        @pl.when(~(has_prev & has_next))
        def _():
            arrived(met.at[k], 2)

    def pass_halo(k):
        @pl.when(takes_halo)
        def _():
            c_halo_mate(k).start()

    def spread_in(i):
        part = x.at[pl.ds(0, 2), pl.ds(piece * i + 1, piece)]
        landed(part, send.at[0], spread.at[i]).wait_recv()

    @pl.when(inner)
    def _():
        @pl.loop(0, LEAD)
        def _(k):
            relay(k)

        @pl.loop(0, chunks)
        def _(k):
            c_y(k).start()

    get_w.wait()
    get_b.wait()
    for t in range(9):
        left, middle, right = (w_ref[3 * t + i] for i in range(3))
        tap = jnp.concatenate([middle, left, right, jnp.zeros_like(left)], axis=0)
        matrix[chans * t : chans * (t + 1)] = tap.T

    bias = b_ref[...].astype(jnp.float32)
    lead = jnp.where(inner, LEAD, 0)

    @pl.loop(0, chunks)
    def _(t):
        @pl.when(t + lead < chunks)
        def _():
            relay(t + lead)

        @pl.when(outer & sends_halo & (t + AHEAD < chunks))
        def _():
            c_halo_own(t + AHEAD).start()

        @pl.when(t >= 1)
        def _():
            meet(t)

        @pl.when((t == 0) & takes_halo)
        def _():
            arrived(met.at[0], 1)

        pass_halo(t)

        @pl.when(lax.rem(t - 1, chunks // PIECES) == 0)
        def _():
            spread_in((t - 1) // (chunks // PIECES))

        @pl.when((t >= 2) & (t < chunks - TAIL + 2))
        def _():
            out_ref[:, pl.ds(ROWS * (t - 2), ROWS)] = convolve(x, matrix, bias, ROWS * (t - 2), ROWS, depth)

    @pl.when(sends_halo)
    def _():
        arrived(met.at[chunks], 2)

    @pl.when(~sends_halo)
    def _():
        arrived(met.at[chunks], 1)

    for kind in range(3):
        sent(kind)

    @pl.when(sends_halo)
    def _():
        sent(3)

    @pl.when(takes_halo)
    def _():
        sent(4)


def finish(done, x, matrix, b_ref, result, tail, sems):
    depth, first, cols, outs = done.shape
    copies = [pltpu.make_async_copy(done.at[z], result.at[z, pl.ds(0, first)], sems.at[z]) for z in range(depth)]
    for copy in copies:
        copy.start()
    bias = b_ref[...].astype(jnp.float32)

    def put(i):
        return pltpu.make_async_copy(
            tail.at[:, pl.ds(ROWS * i, ROWS)],
            result.at[:, pl.ds(first + ROWS * i, ROWS)],
            sems.at[depth + i],
        )

    tail[...] = convolve(x, matrix, bias, first, ROWS * TAIL, depth)
    for i in range(TAIL):
        put(i).start()

    for copy in copies:
        copy.wait()
    for i in range(TAIL):
        put(i).wait()


def body(volume, weights, bias):
    planes, rows, cols, chans = volume.shape
    outs = weights.shape[0]
    slabs = lax.axis_size("slab")
    depth = planes * lax.axis_size("filt")
    taps = weights.transpose(1, 0, 2)
    early = rows - ROWS * TAIL
    flops = 2 * depth * cols * outs * 27 * chans
    done, x, matrix, b = pl.pallas_call(
        functools.partial(kernel, slabs),
        out_shape=[
            pltpu.VMEM((depth, early, cols, outs), jnp.bfloat16),
            pltpu.VMEM((depth + 2, rows + 2, cols, chans), jnp.bfloat16),
            pltpu.VMEM((9 * chans, 4 * outs), jnp.bfloat16),
            pltpu.VMEM((1, outs), jnp.bfloat16),
        ],
        in_specs=[pl.BlockSpec(memory_space=pltpu.HBM)] * 3,
        out_specs=[pl.BlockSpec(memory_space=pltpu.VMEM)] * 4,
        scratch_shapes=[
            pltpu.VMEM(taps.shape, jnp.bfloat16),
            pltpu.SemaphoreType.DMA((5,)),
            pltpu.SemaphoreType.DMA((rows // ROWS,)),
            pltpu.SemaphoreType.DMA((rows // ROWS + 1,)),
            pltpu.SemaphoreType.DMA((2,)),
            pltpu.SemaphoreType.DMA((PIECES,)),
        ],
        compiler_params=pltpu.CompilerParams(
            collective_id=0, has_side_effects=True, vmem_limit_bytes=44 * 1024 * 1024
        ),
        cost_estimate=pl.CostEstimate(
            flops=flops * early, bytes_accessed=16 * rows * cols * chans, transcendentals=0
        ),
    )(volume, taps, bias.reshape(1, outs))
    return pl.pallas_call(
        finish,
        out_shape=jax.ShapeDtypeStruct((depth, rows, cols, outs), jnp.bfloat16),
        in_specs=[pl.BlockSpec(memory_space=pltpu.VMEM)] * 4,
        out_specs=pl.BlockSpec(memory_space=pltpu.HBM),
        scratch_shapes=[
            pltpu.VMEM((depth, ROWS * TAIL, cols, outs), jnp.bfloat16),
            pltpu.SemaphoreType.DMA((depth + TAIL,)),
        ],
        compiler_params=pltpu.CompilerParams(vmem_limit_bytes=16 * 1024 * 1024),
        cost_estimate=pl.CostEstimate(
            flops=flops * ROWS * TAIL, bytes_accessed=4 * depth * rows * cols * outs, transcendentals=0
        ),
    )(done, x, matrix, b)


def solution(mesh):
    return jax.shard_map(
        body,
        mesh=mesh,
        in_specs=(P(("vol", "slab", "filt"), None, None, None), P("filt", None, None), P("filt")),
        out_specs=P(("vol", "slab"), None, None, "filt"),
        check_vma=False,
    )
```

```python
import functools

import jax
import jax.numpy as jnp
from jax import lax
from jax.experimental import pallas as pl
from jax.experimental.pallas import tpu as pltpu
from jax.sharding import PartitionSpec as P

MESH = pl.DeviceIdType.MESH
ROWS = 2
LEAD = 4
AHEAD = 9
TAIL = 2
PIECES = 2


def convolve(x, matrix, bias, row, rows, depth):
    cols, chans = x.shape[2:]
    outs = bias.shape[-1]
    m = depth * rows * cols
    windows = [x[pl.ds(dz, depth), pl.ds(row + dy, rows)].reshape(m, chans) for dz in range(3) for dy in range(3)]
    total = jnp.dot(jnp.concatenate(windows, axis=1), matrix[...], preferred_element_type=jnp.float32)
    place = lax.rem(lax.broadcasted_iota(jnp.int32, (m, 2 * outs), 0), cols)
    near = total[:, : 2 * outs]
    far = total[:, 2 * outs :]
    before = jnp.where(place == 0, 0.0, pltpu.roll(near, 1, 0))
    after = jnp.where(place == cols - 1, 0.0, pltpu.roll(far, m - 1, 0))
    full = near + after + pltpu.roll(before, outs, 1)
    shifted = full[:, :outs] + bias
    result = jnp.where(shifted > 0, shifted, 0.3 * shifted)
    return result.astype(jnp.bfloat16).reshape(depth, rows, cols, outs)


def kernel(slabs, vol_ref, w_hbm, b_hbm, out_ref, x, matrix, b_ref, w_ref, send, over_y, met, params, spread):
    rows, cols, chans = vol_ref.shape[1:]
    depth = out_ref.shape[0]
    chunks = rows // ROWS
    v = lax.axis_index("vol")
    s = lax.axis_index("slab")
    f = lax.axis_index("filt")
    odd = lax.rem(f, 2)
    mate = f + 1 - 2 * odd
    across = lax.rem(f + 2, 4)
    outer = (f == 0) | (f == 3)
    inner = ~outer
    has_prev = s > 0
    has_next = s < slabs - 1
    is_odd = odd == 1
    halo_to = s + 2 * odd - 1
    halo_in = 5 - 5 * odd
    sends_halo = (is_odd & has_next) | (~is_odd & has_prev)
    takes_halo = (is_odd & has_prev) | (~is_odd & has_next)

    to_across = (v, s, across)
    to_mate = (v, s, mate)
    to_halo = (v, halo_to, f)

    def own(k):
        return vol_ref.at[0, pl.ds(ROWS * k, ROWS)]

    def slot(z, k):
        return x.at[z, pl.ds(ROWS * k + 1, ROWS)]

    def remote(src, z, k, kind, sem, dev):
        return pltpu.make_async_remote_copy(
            src_ref=src,
            dst_ref=slot(z, k),
            send_sem=send.at[kind],
            recv_sem=sem,
            device_id=dev,
            device_id_type=MESH,
        )

    def c_y(k):
        return remote(own(k), f + 1, k, 0, over_y.at[k], to_across)

    def c_fwd(k):
        return remote(slot(across + 1, k), across + 1, k, 2, met.at[k + 1], to_mate)

    def c_halo_own(k):
        return remote(own(k), halo_in, k, 3, met.at[k], to_halo)

    def c_halo_fwd(k):
        return remote(slot(across + 1, k), halo_in, k, 3, met.at[k], to_halo)

    def c_halo_mate(k):
        return remote(slot(halo_in, k), halo_in, k, 4, met.at[k + 1], to_mate)

    piece = rows // PIECES

    def c_local(i):
        part = pl.ds(piece * i, piece)
        return pltpu.make_async_copy(
            vol_ref.at[0, part], x.at[f + 1, pl.ds(piece * i + 1, piece)], spread.at[i]
        )

    def c_core(i):
        part = pl.ds(piece * i, piece)
        return pltpu.make_async_remote_copy(
            src_ref=vol_ref.at[0, part],
            dst_ref=x.at[f + 1, pl.ds(piece * i + 1, piece)],
            send_sem=send.at[1],
            recv_sem=spread.at[i],
            device_id=to_mate,
            device_id_type=MESH,
        )

    def landed(ref, send_sem, recv_sem):
        return pltpu.make_async_remote_copy(
            src_ref=ref, dst_ref=ref, send_sem=send_sem, recv_sem=recv_sem, device_id=to_mate, device_id_type=MESH
        )

    def arrived(sem, planes):
        part = x.at[pl.ds(0, planes), pl.ds(1, ROWS)]
        landed(part, send.at[0], sem).wait_recv()

    def sent(kind):
        landed(x.at[0, pl.ds(1, rows)], send.at[kind], over_y.at[0]).wait_send()

    get_w = pltpu.make_async_copy(w_hbm, w_ref, params.at[0])
    get_b = pltpu.make_async_copy(b_hbm, b_ref, params.at[1])
    get_w.start()
    get_b.start()

    barrier = pltpu.get_barrier_semaphore()
    pl.semaphore_signal(barrier, inc=1, device_id=to_mate, device_id_type=MESH)
    pl.semaphore_signal(barrier, inc=1, device_id=to_across, device_id_type=MESH)

    @pl.when(has_prev)
    def _():
        pl.semaphore_signal(barrier, inc=1, device_id=(v, s - 1, f), device_id_type=MESH)

    @pl.when(has_next)
    def _():
        pl.semaphore_signal(barrier, inc=1, device_id=(v, s + 1, f), device_id_type=MESH)

    greeted = 2 + has_prev.astype(jnp.int32) + has_next.astype(jnp.int32)
    pl.semaphore_wait(barrier, greeted)

    @pl.when(outer)
    def _():
        @pl.loop(0, chunks)
        def _(k):
            c_y(k).start()

            @pl.when(sends_halo & (k < AHEAD))
            def _():
                c_halo_own(k).start()

            @pl.when(k == 1)
            def _():
                for i in range(PIECES):
                    c_core(i).start()
                    c_local(i).start()

    @pl.when(inner)
    def _():
        for i in range(PIECES):
            c_core(i).start()
            c_local(i).start()

    zero_row = jnp.zeros((cols, chans), x.dtype)
    for z in range(depth + 2):
        x[z, 0] = zero_row
        x[z, rows + 1] = zero_row

    def clear(z):
        @pl.loop(1, rows + 1)
        def _(r):
            x[z, r] = zero_row

    @pl.when(~has_prev)
    def _():
        clear(0)

    @pl.when(~has_next)
    def _():
        clear(depth + 1)

    def relay(k):
        arrived(over_y.at[k], 1)
        c_fwd(k).start()

        @pl.when(inner & sends_halo)
        def _():
            c_halo_fwd(k).start()

    def meet(k):
        @pl.when(has_prev & has_next)
        def _():
            arrived(met.at[k], 3)

        @pl.when(~(has_prev & has_next))
        def _():
            arrived(met.at[k], 2)

    def pass_halo(k):
        @pl.when(takes_halo)
        def _():
            c_halo_mate(k).start()

    def spread_in(i):
        part = x.at[pl.ds(0, 2), pl.ds(piece * i + 1, piece)]
        landed(part, send.at[0], spread.at[i]).wait_recv()

    get_w.wait()
    get_b.wait()
    for t in range(9):
        left, middle, right = (w_ref[3 * t + i] for i in range(3))
        tap = jnp.concatenate([middle, left, right, jnp.zeros_like(left)], axis=0)
        matrix[chans * t : chans * (t + 1)] = tap.T

    @pl.when(inner)
    def _():
        @pl.loop(0, LEAD)
        def _(k):
            relay(k)

        @pl.loop(0, chunks)
        def _(k):
            c_y(k).start()

    bias = b_ref[...].astype(jnp.float32)
    lead = jnp.where(inner, LEAD, 0)

    @pl.loop(0, chunks)
    def _(t):
        @pl.when(t + lead < chunks)
        def _():
            relay(t + lead)

        @pl.when(outer & sends_halo & (t + AHEAD < chunks))
        def _():
            c_halo_own(t + AHEAD).start()

        @pl.when(t >= 1)
        def _():
            meet(t)

        @pl.when((t == 0) & takes_halo)
        def _():
            arrived(met.at[0], 1)

        pass_halo(t)

        @pl.when(lax.rem(t - 1, chunks // PIECES) == 0)
        def _():
            spread_in((t - 1) // (chunks // PIECES))

        @pl.when((t >= 2) & (t < chunks - TAIL + 2))
        def _():
            out_ref[:, pl.ds(ROWS * (t - 2), ROWS)] = convolve(x, matrix, bias, ROWS * (t - 2), ROWS, depth)

    @pl.when(sends_halo)
    def _():
        arrived(met.at[chunks], 2)

    @pl.when(~sends_halo)
    def _():
        arrived(met.at[chunks], 1)

    for kind in range(3):
        sent(kind)

    @pl.when(sends_halo)
    def _():
        sent(3)

    @pl.when(takes_halo)
    def _():
        sent(4)


def finish(done, x, matrix, b_ref, result, tail, sems):
    depth, first, cols, outs = done.shape
    copies = [pltpu.make_async_copy(done.at[z], result.at[z, pl.ds(0, first)], sems.at[z]) for z in range(depth)]
    for copy in copies:
        copy.start()
    bias = b_ref[...].astype(jnp.float32)

    def put(i):
        return pltpu.make_async_copy(
            tail.at[:, pl.ds(ROWS * i, ROWS)],
            result.at[:, pl.ds(first + ROWS * i, ROWS)],
            sems.at[depth + i],
        )

    tail[...] = convolve(x, matrix, bias, first, ROWS * TAIL, depth)
    for i in range(TAIL):
        put(i).start()

    for copy in copies:
        copy.wait()
    for i in range(TAIL):
        put(i).wait()


def body(volume, weights, bias):
    planes, rows, cols, chans = volume.shape
    outs = weights.shape[0]
    slabs = lax.axis_size("slab")
    depth = planes * lax.axis_size("filt")
    taps = weights.transpose(1, 0, 2)
    early = rows - ROWS * TAIL
    flops = 2 * depth * cols * outs * 27 * chans
    done, x, matrix, b = pl.pallas_call(
        functools.partial(kernel, slabs),
        out_shape=[
            pltpu.VMEM((depth, early, cols, outs), jnp.bfloat16),
            pltpu.VMEM((depth + 2, rows + 2, cols, chans), jnp.bfloat16),
            pltpu.VMEM((9 * chans, 4 * outs), jnp.bfloat16),
            pltpu.VMEM((1, outs), jnp.bfloat16),
        ],
        in_specs=[pl.BlockSpec(memory_space=pltpu.HBM)] * 3,
        out_specs=[pl.BlockSpec(memory_space=pltpu.VMEM)] * 4,
        scratch_shapes=[
            pltpu.VMEM(taps.shape, jnp.bfloat16),
            pltpu.SemaphoreType.DMA((5,)),
            pltpu.SemaphoreType.DMA((rows // ROWS,)),
            pltpu.SemaphoreType.DMA((rows // ROWS + 1,)),
            pltpu.SemaphoreType.DMA((2,)),
            pltpu.SemaphoreType.DMA((PIECES,)),
        ],
        compiler_params=pltpu.CompilerParams(
            collective_id=0, has_side_effects=True, vmem_limit_bytes=44 * 1024 * 1024
        ),
        cost_estimate=pl.CostEstimate(
            flops=flops * early, bytes_accessed=16 * rows * cols * chans, transcendentals=0
        ),
    )(volume, taps, bias.reshape(1, outs))
    return pl.pallas_call(
        finish,
        out_shape=jax.ShapeDtypeStruct((depth, rows, cols, outs), jnp.bfloat16),
        in_specs=[pl.BlockSpec(memory_space=pltpu.VMEM)] * 4,
        out_specs=pl.BlockSpec(memory_space=pltpu.HBM),
        scratch_shapes=[
            pltpu.VMEM((depth, ROWS * TAIL, cols, outs), jnp.bfloat16),
            pltpu.SemaphoreType.DMA((depth + TAIL,)),
        ],
        compiler_params=pltpu.CompilerParams(vmem_limit_bytes=16 * 1024 * 1024),
        cost_estimate=pl.CostEstimate(
            flops=flops * ROWS * TAIL, bytes_accessed=4 * depth * rows * cols * outs, transcendentals=0
        ),
    )(done, x, matrix, b)


def solution(mesh):
    return jax.shard_map(
        body,
        mesh=mesh,
        in_specs=(P(("vol", "slab", "filt"), None, None, None), P("filt", None, None), P("filt")),
        out_specs=P(("vol", "slab"), None, None, "filt"),
        check_vma=False,
    )
```
